512 devices in a mesh: replica: 64 (over y, z), tensor: 8 (over x, core).
Axes of the slice: x: 4, y: 4, z: 16, core: 2. Of those that a mesh axis runs over, the one named last changes fastest.
Arguments:
- prefill_q: bfloat16 [24576, 8192], P('replica', 'tensor'), may hold values from -16 to 16
- decode_q: bfloat16 [128, 8192], P('replica', 'tensor'), may hold values from -16 to 16
- overflow_q: bfloat16 [1536, 8192], P('replica', 'tensor'), may hold values from -16 to 16
- key_pool: bfloat16 [417792, 1024], P('replica', 'tensor'), may hold values from -10 to 10
- value_pool: bfloat16 [417792, 1024], P('replica', 'tensor'), may hold values from -6 to 6
- prefill_pages: int32 [64, 19], P('replica'), may hold values from 0 to 50, as said below
- decode_pages: int32 [128, 4], P('replica'), may hold values from 0 to 50, as said below
- decode_len: int32 [128], P('replica'), may hold values from 1 to 512, as said below
- overflow_pages: int32 [1536], P('replica'), may hold values from 0 to 50, as said below
- overflow_len: int32 [1536], P('replica'), may hold values from 1 to 128, as said below
- overflow_dest: int32 [1536], P('replica'), may hold values from 0 to 63, as said below
Outputs:
- prefill_out: bfloat16 [24576, 8192], P(('replica', 'tensor'))
- decode_out: bfloat16 [128, 8192], P('replica', 'tensor')
- moved_out: bfloat16 [4096, 8192], P('replica', 'tensor')
The draws below stay inside these ranges and needn't reach their ends.
Inputs may be any that keep to these rules, and one draw needn't show every extreme that they name: The page lists of one replica (prefill_pages, decode_pages and overflow_pages together) name distinct pages of that replica's pool. `decode_pages`: distinct pages of the own pool, as for prefill_pages. `overflow_pages`: distinct pages of the own pool, as for prefill_pages. `decode_len`: every replica has a decoding request of exactly 512 positions. `overflow_len`: every replica has an overflow request of exactly 128 positions. `overflow_dest`: the requests of one replica go to distinct replicas other than itself; one replica receives a request from every other replica.
All inputs are finite; a program needn't handle non-finite values.
Results may differ from the reference program's by a relative error of at most 0.0049.
Values may be sent and summed in bfloat16 or wider, within the bound.
A program may use at most 64 MiB of HBM per device.

```python
import math
import jax
import jax.numpy as jnp
from jax import lax

Q_HEADS = 64
KV_HEADS = 8
D_HEAD = 128
PAGE = 128
STRETCH = 384
PRIOR = 16
DEC = 2
DEC_PAGES = 4
OVERFLOW = 24
PRE_PAGES = 19
POOL = 51
N_REPLICA = 64


def query_draw(key, salt, count):
    noise = 2.5 * jax.random.normal(jax.random.fold_in(key, salt), (count, Q_HEADS * D_HEAD), jnp.float32)
    return jnp.clip(noise, -16.0, 16.0).astype(jnp.bfloat16)


def draw_prefill_q(key, part):
    return query_draw(key, 301, N_REPLICA * STRETCH)


def draw_decode_q(key, part):
    return query_draw(key, 311, N_REPLICA * DEC)


def draw_overflow_q(key, part):
    return query_draw(key, 321, N_REPLICA * OVERFLOW)


def draw_key_pool(key, part):
    total = N_REPLICA * POOL * PAGE
    noise = jax.random.normal(jax.random.fold_in(key, 201), (total, KV_HEADS * D_HEAD), jnp.float32)
    return jnp.clip(noise, -10.0, 10.0).astype(jnp.bfloat16)


def pool_orders(key):
    seeds = jax.random.split(jax.random.fold_in(key, 11), N_REPLICA)
    return jax.vmap(lambda k: jax.random.permutation(k, POOL))(seeds).astype(jnp.int32)


def draw_prefill_pages(key, part):
    return pool_orders(key)[:, :PRE_PAGES]


def draw_decode_pages(key, part):
    return pool_orders(key)[:, PRE_PAGES:PRE_PAGES + DEC * DEC_PAGES].reshape(N_REPLICA * DEC, DEC_PAGES)


def draw_overflow_pages(key, part):
    return pool_orders(key)[:, PRE_PAGES + DEC * DEC_PAGES:].reshape(N_REPLICA * OVERFLOW)


def ragged(key, salt, count, most):
    base = jax.random.randint(jax.random.fold_in(key, salt), (N_REPLICA, count), 1, most + 1)
    spot = jax.random.randint(jax.random.fold_in(key, salt + 1), (N_REPLICA, 1), 0, count)
    filled = jnp.where(jnp.arange(count)[None, :] == spot, most, base)
    return filled.reshape(-1).astype(jnp.int32)


def draw_decode_len(key, part):
    return ragged(key, 21, DEC, DEC_PAGES * PAGE)


def draw_overflow_len(key, part):
    return ragged(key, 25, OVERFLOW, PAGE)


def draw_overflow_dest(key, part):
    busiest = jax.random.randint(jax.random.fold_in(key, 31), (), 0, N_REPLICA)
    source = jnp.arange(N_REPLICA, dtype=jnp.int32)
    seeds = jax.random.split(jax.random.fold_in(key, 32), N_REPLICA)
    offsets = jax.vmap(lambda k: jax.random.permutation(k, N_REPLICA - 1))(seeds).astype(jnp.int32)
    forced = ((busiest - source - 1) % N_REPLICA)[:, None]
    column = jnp.arange(N_REPLICA - 1, dtype=jnp.int32)[None, :]
    place = jax.random.randint(jax.random.fold_in(key, 33), (N_REPLICA, 1), 0, OVERFLOW)
    displaced = jnp.take_along_axis(offsets, place, axis=1)
    swapped = jnp.where(offsets == forced, displaced, jnp.where(column == place, forced, offsets))
    chosen = jnp.where((source == busiest)[:, None], offsets, swapped)[:, :OVERFLOW]
    return ((source[:, None] + 1 + chosen) % N_REPLICA).reshape(-1).astype(jnp.int32)


def block_scale(stream_key, extent, pieces, low, largest):
    loudness, own = 1.0, jax.random.fold_in(stream_key, 6)
    for position, shards_of in pieces:
        steps = jnp.exp(jax.random.uniform(jax.random.fold_in(own, position), (shards_of,), jnp.float32, low / len(pieces), largest / len(pieces)))
        loudness = loudness * jnp.repeat(steps, extent[position] // shards_of).reshape([-1 if axis == position else 1 for axis in range(len(extent))])
    return loudness


def centred(own_key, shape, scale, most, pieces=(), kind=jnp.bfloat16):
    gain = block_scale(own_key, shape, pieces, -0.22, 0.18) if pieces else 1.0
    array = jax.random.normal(own_key, shape, jnp.float32) * scale * gain
    return jnp.minimum(jnp.maximum(array, -most), most).astype(kind)


def setup_inputs(seed: int = 0) -> dict:
    key_of = jax.random.split(jax.random.key(seed), 12)
    return {
        "prefill_q": draw_prefill_q(jax.random.fold_in(key_of[11], 71), 0),
        "decode_q": draw_decode_q(jax.random.fold_in(key_of[11], 71), 0),
        "overflow_q": draw_overflow_q(jax.random.fold_in(key_of[11], 71), 0),
        "key_pool": draw_key_pool(jax.random.fold_in(key_of[11], 71), 0),
        "value_pool": centred(key_of[4], (N_REPLICA * POOL * PAGE, KV_HEADS * D_HEAD), 1.0, 6.0, ((0, 64), (1, 8))),
        "prefill_pages": draw_prefill_pages(jax.random.fold_in(key_of[11], 71), 0),
        "decode_pages": draw_decode_pages(jax.random.fold_in(key_of[11], 71), 0),
        "decode_len": draw_decode_len(jax.random.fold_in(key_of[11], 71), 0),
        "overflow_pages": draw_overflow_pages(jax.random.fold_in(key_of[11], 71), 0),
        "overflow_len": draw_overflow_len(jax.random.fold_in(key_of[11], 71), 0),
        "overflow_dest": draw_overflow_dest(jax.random.fold_in(key_of[11], 71), 0),
    }


def attend_block(queries, key_rows, value_rows, usable):
    per_group = Q_HEADS // KV_HEADS
    count = queries.shape[0]
    q_four = queries.astype(jnp.float32).reshape(count, KV_HEADS, per_group, D_HEAD)
    k_three = key_rows.astype(jnp.float32).reshape(-1, KV_HEADS, D_HEAD)
    v_three = value_rows.astype(jnp.float32).reshape(-1, KV_HEADS, D_HEAD)
    scores = jnp.einsum('ngqd,lgd->gqnl', q_four, k_three) / math.sqrt(D_HEAD)
    scores = jnp.where(usable[None, None], scores, -1e+30)
    maxima = lax.optimization_barrier(jnp.max(scores, axis=-1, keepdims=True))
    expon = jnp.exp(scores - maxima)
    weights = (expon / lax.optimization_barrier(jnp.sum(expon, axis=-1, keepdims=True))).astype(jnp.bfloat16)
    result = jnp.einsum('gqnl,lgd->ngqd', weights.astype(jnp.float32), v_three)
    return result.reshape(count, -1).astype(jnp.bfloat16)

def attend_single(query_row, key_rows, value_rows, usable):
    return attend_block(query_row[None], key_rows, value_rows, usable[None])[0]

def reference(prefill_q, decode_q, overflow_q, key_pool, value_pool, prefill_pages, decode_pages, decode_len, overflow_pages, overflow_len, overflow_dest):
    width_kv = KV_HEADS * D_HEAD
    width_q = Q_HEADS * D_HEAD
    key_parts = key_pool.reshape(N_REPLICA, POOL, PAGE, width_kv)
    value_parts = value_pool.reshape(N_REPLICA, POOL, PAGE, width_kv)
    key_span = PRE_PAGES * PAGE
    causal = jnp.arange(key_span)[None, :] <= (PRIOR * PAGE + jnp.arange(STRETCH))[:, None]

    def prefill_replica(inputs):
        queries, key_pages, value_pages, page_list = inputs
        key_rows = key_pages[page_list].reshape(key_span, width_kv)
        value_rows = value_pages[page_list].reshape(key_span, width_kv)
        return attend_block(queries, key_rows, value_rows, causal)
    prefill_out = lax.map(prefill_replica, (prefill_q.reshape(N_REPLICA, STRETCH, width_q), key_parts, value_parts, prefill_pages))
    prefill_out = prefill_out.reshape(N_REPLICA * STRETCH, width_q)

    def decode_replica(inputs):
        queries, key_pages, value_pages, listed_pages, lengths = inputs
        key_rows = key_pages[listed_pages].reshape(DEC, DEC_PAGES * PAGE, width_kv)
        value_rows = value_pages[listed_pages].reshape(DEC, DEC_PAGES * PAGE, width_kv)
        usable = jnp.arange(DEC_PAGES * PAGE)[None, :] < lengths[:, None]
        return jax.vmap(attend_single)(queries, key_rows, value_rows, usable)
    decode_out = lax.map(decode_replica, (decode_q.reshape(N_REPLICA, DEC, width_q), key_parts, value_parts, decode_pages.reshape(N_REPLICA, DEC, DEC_PAGES), decode_len.reshape(N_REPLICA, DEC)))
    decode_out = decode_out.reshape(N_REPLICA * DEC, width_q)

    def overflow_replica(inputs):
        queries, key_pages, value_pages, page_ids, lengths = inputs
        key_rows = key_pages[page_ids]
        value_rows = value_pages[page_ids]
        usable = jnp.arange(PAGE)[None, :] < lengths[:, None]
        return jax.vmap(attend_single)(queries, key_rows, value_rows, usable)
    moved = lax.map(overflow_replica, (overflow_q.reshape(N_REPLICA, OVERFLOW, width_q), key_parts, value_parts, overflow_pages.reshape(N_REPLICA, OVERFLOW), overflow_len.reshape(N_REPLICA, OVERFLOW)))
    target = overflow_dest.reshape(N_REPLICA, OVERFLOW) * N_REPLICA + jnp.arange(N_REPLICA, dtype=jnp.int32)[:, None]
    moved_out = jnp.zeros((N_REPLICA * N_REPLICA, width_q), jnp.bfloat16)
    moved_out = moved_out.at[target.reshape(-1).astype(jnp.int32)].set(moved.reshape(-1, width_q))
    return (prefill_out, decode_out, moved_out)
```

```python
import functools
import math

import jax
import jax.numpy as jnp
from jax import lax
from jax.experimental import pallas as pl
from jax.experimental.pallas import tpu as pltpu
from jax.sharding import PartitionSpec as P

D = 128
PAGE = 128
GROUP = 8
SCALE = math.log2(math.e) / math.sqrt(D)
NEG = -1e30
CHUNK = 1024
MESH = pl.DeviceIdType.MESH
BF16 = jnp.bfloat16
F32 = jnp.float32


def tiles(x):
    return [x[:, i : i + 128] for i in range(0, x.shape[1], 128)]


def dot_t(a, b):
    return lax.dot_general(a, b, (((1,), (1,)), ((), ())), preferred_element_type=F32)


def iota(shape, axis):
    return lax.broadcasted_iota(jnp.int32, shape, axis)


def kernel(
    sizes,
    prefill_pages,
    decode_pages,
    decode_len,
    overflow_pages,
    overflow_len,
    overflow_dest,
    prefill_q,
    decode_q,
    overflow_q,
    key_pool,
    value_pool,
    prefill_out,
    decode_out,
    moved_out,
    keys,
    values,
    queries,
    small_q,
    small_rows,
    key_rows,
    value_rows,
    score_a,
    score_b,
    blocks,
    send_rows,
    got_rows,
    wide_rows,
    in_sem,
    block_send,
    block_recv,
    own_sem,
    row_send,
    row_recv,
):
    n_rep, n_ten = sizes
    me_r, me_t = lax.axis_index("replica"), lax.axis_index("tensor")
    span = key_rows.shape[0]
    tokens = queries.shape[0]
    part = tokens // n_ten
    pair = 2 * part
    rows = pair * GROUP
    prior = span - tokens
    chips = n_ten // 2

    loads = [
        pltpu.make_async_copy(source, target, in_sem.at[i])
        for i, (source, target) in enumerate(
            (
                (overflow_q, small_q),
                (key_pool, keys),
                (value_pool, values),
                (prefill_q, queries),
            )
        )
    ]
    for load in loads:
        load.start()

    barrier = pltpu.get_barrier_semaphore()

    def greet_replica(i, _):
        pl.semaphore_signal(
            barrier, inc=1, device_id={"replica": lax.rem(me_r + i, n_rep)}, device_id_type=MESH
        )
        return 0

    def greet_tensor(i, _):
        pl.semaphore_signal(
            barrier, inc=1, device_id={"tensor": lax.rem(me_t + i, n_ten)}, device_id_type=MESH
        )
        return 0

    lax.fori_loop(1, n_rep, greet_replica, 0)
    lax.fori_loop(1, n_ten, greet_tensor, 0)

    loads[0].wait()
    n_over = overflow_q.shape[0]
    n_dec = decode_q.shape[0]
    small_rows[0:n_over, :] = small_q[...].astype(F32)
    small_rows[n_over:, :] = jnp.zeros((8, GROUP * D), F32)
    small_rows[n_over : n_over + n_dec, :] = decode_q[...].astype(F32)
    loads[1].wait()
    loads[2].wait()

    row_slot = iota((64, 128), 0) % 8
    lane = iota((64, 128), 1)
    dec_pages = decode_pages.shape[1]
    attended = []
    for g in range(n_over // 8 + 1):
        q = jnp.concatenate(
            [small_rows[g * 8 : (g + 1) * 8, h * D : (h + 1) * D] for h in range(GROUP)], axis=0
        ).astype(BF16)
        pages, owner, limit = [], [], []
        for i in range(8):
            if g < n_over // 8:
                pages.append(overflow_pages[g * 8 + i])
                owner.append(i)
                limit.append(overflow_len[g * 8 + i])
            else:
                pages.append(decode_pages[i // dec_pages, i % dec_pages])
                owner.append(i // dec_pages)
                limit.append(decode_len[i // dec_pages] - (i % dec_pages) * PAGE)
        k = jnp.concatenate([keys[p] for p in pages], axis=0)
        v = jnp.concatenate([values[p] for p in pages], axis=0)
        s = tiles(dot_t(q, k))
        s = [
            jnp.where((row_slot == owner[i]) & (lane < limit[i]), s[i] * SCALE, NEG)
            for i in range(8)
        ]
        m = jnp.max(functools.reduce(jnp.maximum, s), axis=1, keepdims=True)
        p = [jnp.exp2(x - m) for x in s]
        total = jnp.sum(functools.reduce(jnp.add, p), axis=1, keepdims=True)
        o = jnp.dot(
            jnp.concatenate([x.astype(BF16) for x in p], axis=1), v, preferred_element_type=F32
        )
        attended.append((o / total).astype(BF16))
    last = attended[-1].astype(F32)
    for h in range(GROUP):
        decode_out[:, h * D : (h + 1) * D] = last[h * 8 : h * 8 + n_dec, :].astype(BF16)

    width = 64 * (n_over // 8)
    column = iota((1, width), 1)
    request = (column // 64) * 8 + column % 8
    dest = jnp.full((1, width), -1, jnp.int32)
    for j in range(n_over):
        dest = jnp.where(request == j, overflow_dest[j], dest)
    target = iota((n_rep * 8, width), 0)
    pick = (dest * 8 + (column // 8) % 8 == target).astype(F32).astype(BF16)
    sent = jnp.dot(pick, jnp.concatenate(attended[:-1], axis=0), preferred_element_type=F32)
    send_rows[...] = sent.reshape(n_rep, 8, D).astype(BF16)
    got_rows[me_r] = send_rows[me_r]

    pl.semaphore_wait(barrier, n_rep + n_ten - 2)

    def send_row(i, _):
        to = lax.rem(me_r + i, n_rep)
        pltpu.make_async_remote_copy(
            src_ref=send_rows.at[to],
            dst_ref=got_rows.at[me_r],
            send_sem=row_send,
            recv_sem=row_recv,
            device_id={"replica": to},
            device_id_type=MESH,
        ).start()
        return 0

    lax.fori_loop(1, n_rep, send_row, 0)

    def gather(i, _):
        at = pl.ds(pl.multiple_of(i * PAGE, PAGE), PAGE)
        listed = prefill_pages[0, i]
        page = keys[listed]
        key_rows[at, 0:D] = page
        key_rows[at, D : 2 * D] = page
        value_rows[at, 0:D] = values[listed]
        value_rows[at, D : 2 * D] = jnp.ones((PAGE, D), BF16)
        return 0

    lax.fori_loop(0, span // PAGE, gather, 0)
    loads[3].wait()

    chunks = [(o, min(CHUNK, span - o)) for o in range(0, span, CHUNK)]
    scratch = (score_a, score_b)
    me_x = me_t // 2

    def block_copy(at, to):
        offset = pl.multiple_of((to % 2) * part, 16)
        return pltpu.make_async_remote_copy(
            src_ref=blocks.at[at, pl.ds(offset, part), :],
            dst_ref=prefill_out.at[:, pl.ds(pl.multiple_of(me_t * GROUP * D, GROUP * D), GROUP * D)],
            send_sem=block_send.at[to],
            recv_sem=block_recv.at[me_t],
            device_id={"tensor": to},
            device_id_type=MESH,
        )

    def block(step, _):
        ahead = jnp.where(step < 2, 2 - step, 9 - 3 * step)
        chip = lax.rem(me_x + ahead, chips)
        at = pl.ds(pl.multiple_of(chip * pair, pair), pair)
        q = jnp.concatenate([queries[at, h * D : (h + 1) * D] for h in range(GROUP)], axis=0)
        q = q.astype(F32) * SCALE
        high = q.astype(BF16)
        q = jnp.concatenate([high, (q - high.astype(F32)).astype(BF16)], axis=1)
        peak = [None] * len(chunks)

        def scores(j):
            o, w = chunks[j]
            s = dot_t(q, key_rows[o : o + w, :])
            if o + w > prior:
                token = iota((rows, w), 0) % pair + chip * pair
                s = jnp.where(iota((rows, w), 1) + (o - prior) <= token, s, NEG)
            m = jnp.max(functools.reduce(jnp.maximum, tiles(s)), axis=1, keepdims=True)
            m = jnp.broadcast_to(m, (rows, 128))
            peak[j] = m if j == 0 else jnp.maximum(peak[j - 1], m)
            scratch[j % 2][:, :w] = s

        def weigh(j, acc):
            o, w = chunks[j]
            p = [jnp.exp2(x - peak[j]).astype(BF16) for x in tiles(scratch[j % 2][:, :w])]
            o = jnp.dot(
                jnp.concatenate(p, axis=1), value_rows[o : o + w, :], preferred_element_type=F32
            )
            if acc is None:
                return o
            shrink = jnp.exp2(peak[j - 1] - peak[j])
            return jnp.concatenate([x * shrink for x in tiles(acc)], axis=1) + o

        acc = None
        for j in range(len(chunks) + 1):
            if j < len(chunks):
                scores(j)
            if j > 0:
                acc = weigh(j - 1, acc)
        out = (acc[:, :D] / acc[:, D:]).astype(BF16)
        for h in range(GROUP):
            blocks[step, :, h * D : (h + 1) * D] = out[h * pair : (h + 1) * pair, :]

        for core in range(2):
            to = chip * 2 + core

            @pl.when(to != me_t)
            def _():
                block_copy(step, to).start()

        return 0

    lax.fori_loop(0, chips, block, 0)

    own = pltpu.make_async_copy(
        blocks.at[chips - 1, pl.ds(pl.multiple_of((me_t % 2) * part, 16), part), :],
        prefill_out.at[:, pl.ds(pl.multiple_of(me_t * GROUP * D, GROUP * D), GROUP * D)],
        own_sem,
    )
    own.start()

    pltpu.make_async_copy(got_rows.at[0 : n_rep - 1], got_rows.at[0 : n_rep - 1], row_recv).wait()
    pltpu.make_async_copy(send_rows.at[0 : n_rep - 1], send_rows.at[0 : n_rep - 1], row_send).wait()
    wide_rows[...] = got_rows[...].astype(F32).reshape(n_rep * 8, D)
    for h in range(GROUP):
        moved_out[:, h * D : (h + 1) * D] = wide_rows[pl.ds(h, n_rep, stride=8), :].astype(BF16)

    own.wait()

    def finish(i, _):
        other = lax.rem(me_t + i, n_ten)
        arrived = prefill_out.at[
            :, pl.ds(pl.multiple_of(other * GROUP * D, GROUP * D), GROUP * D)
        ]
        pltpu.make_async_copy(arrived, arrived, block_recv.at[other]).wait()
        left = blocks.at[0, 0:part, :]
        pltpu.make_async_copy(left, left, block_send.at[other]).wait()
        return 0

    lax.fori_loop(1, n_ten, finish, 0)


def per_device(
    prefill_q,
    decode_q,
    overflow_q,
    key_pool,
    value_pool,
    prefill_pages,
    decode_pages,
    decode_len,
    overflow_pages,
    overflow_len,
    overflow_dest,
):
    n_rep, n_ten = lax.axis_size("replica"), lax.axis_size("tensor")
    tokens, width = prefill_q.shape
    span = prefill_pages.shape[1] * PAGE
    rows = 2 * tokens // n_ten * GROUP
    n_over = overflow_q.shape[0]
    key_pool = key_pool.reshape(-1, PAGE, D)
    value_pool = value_pool.reshape(-1, PAGE, D)
    smem = pl.BlockSpec(memory_space=pltpu.SMEM)
    vmem = pl.BlockSpec(memory_space=pltpu.VMEM)
    hbm = pl.BlockSpec(memory_space=pl.ANY)
    return pl.pallas_call(
        functools.partial(kernel, (n_rep, n_ten)),
        out_shape=(
            jax.ShapeDtypeStruct((tokens // n_ten, width * n_ten), BF16),
            jax.ShapeDtypeStruct(decode_q.shape, BF16),
            jax.ShapeDtypeStruct((n_rep, width), BF16),
        ),
        in_specs=[smem] * 6 + [hbm, vmem, hbm, hbm, hbm],
        out_specs=(hbm, vmem, vmem),
        scratch_shapes=[
            pltpu.VMEM(key_pool.shape, BF16),
            pltpu.VMEM(key_pool.shape, BF16),
            pltpu.VMEM((tokens, width), BF16),
            pltpu.VMEM((n_over, width), BF16),
            pltpu.VMEM((n_over + 8, width), F32),
            pltpu.VMEM((span, 2 * D), BF16),
            pltpu.VMEM((span, 2 * D), BF16),
            pltpu.VMEM((rows, CHUNK), F32),
            pltpu.VMEM((rows, CHUNK), F32),
            pltpu.VMEM((n_ten // 2, 2 * tokens // n_ten, width), BF16),
            pltpu.VMEM((n_rep, 8, D), BF16),
            pltpu.VMEM((n_rep, 8, D), BF16),
            pltpu.VMEM((n_rep * 8, D), F32),
            pltpu.SemaphoreType.DMA((4,)),
            pltpu.SemaphoreType.DMA((n_ten,)),
            pltpu.SemaphoreType.DMA((n_ten,)),
            pltpu.SemaphoreType.DMA,
            pltpu.SemaphoreType.DMA,
            pltpu.SemaphoreType.DMA,
        ],
        compiler_params=pltpu.CompilerParams(
            collective_id=0, has_side_effects=True, vmem_limit_bytes=56 << 20
        ),
    )(
        prefill_pages,
        decode_pages,
        decode_len,
        overflow_pages,
        overflow_len,
        overflow_dest,
        prefill_q,
        decode_q,
        overflow_q,
        key_pool,
        value_pool,
    )


def solution(mesh):
    both = P("replica", "tensor")
    in_specs = (both,) * 5 + (P("replica", None),) * 2 + (P("replica"),) * 4
    out_specs = (P(("replica", "tensor"), None), both, both)
    return jax.shard_map(
        per_device, mesh=mesh, in_specs=in_specs, out_specs=out_specs, check_vma=False
    )
```

```python
import functools
import math

import jax
import jax.numpy as jnp
from jax import lax
from jax.experimental import pallas as pl
from jax.experimental.pallas import tpu as pltpu
from jax.sharding import PartitionSpec as P

D = 128
PAGE = 128
GROUP = 8
SCALE = math.log2(math.e) / math.sqrt(D)
NEG = -1e30
CHUNK = 1024
ATTEND_VMEM = 24 << 20
PLACE_VMEM = 8 << 20
MESH = pl.DeviceIdType.MESH
BF16 = jnp.bfloat16
F32 = jnp.float32


def tiles(x):
    return [x[:, i : i + 128] for i in range(0, x.shape[1], 128)]


def dot_t(a, b):
    return lax.dot_general(a, b, (((1,), (1,)), ((), ())), preferred_element_type=F32)


def iota(shape, axis):
    return lax.broadcasted_iota(jnp.int32, shape, axis)


def kernel(
    sizes,
    prefill_pages_hbm,
    decode_pages_hbm,
    decode_len_hbm,
    overflow_pages_hbm,
    overflow_len_hbm,
    overflow_dest_hbm,
    prefill_q,
    decode_q,
    overflow_q,
    key_pool,
    value_pool,
    prefill_out,
    decode_out,
    moved_rows,
    prefill_pages,
    decode_pages,
    decode_len,
    overflow_pages,
    overflow_len,
    overflow_dest,
    decode_held,
    keys,
    values,
    queries,
    small_q,
    small_rows,
    key_rows,
    value_rows,
    score_a,
    score_b,
    blocks,
    send_rows,
    table_sem,
    in_sem,
    block_send,
    block_recv,
    own_sem,
    kept_sem,
    row_send,
    row_recv,
):
    n_rep, n_ten, depth_z = sizes
    me_r, me_t = lax.axis_index("replica"), lax.axis_index("tensor")
    span = key_rows.shape[0]
    tokens = queries.shape[0]
    part = tokens // n_ten
    pair = 2 * part
    rows = pair * GROUP
    prior = span - tokens
    chips = n_ten // 2

    tables = [
        pltpu.make_async_copy(source, target, table_sem.at[i])
        for i, (source, target) in enumerate(
            (
                (prefill_pages_hbm, prefill_pages),
                (decode_pages_hbm, decode_pages),
                (decode_len_hbm, decode_len),
                (overflow_pages_hbm, overflow_pages),
                (overflow_len_hbm, overflow_len),
                (overflow_dest_hbm, overflow_dest),
                (decode_q, decode_held),
            )
        )
    ]
    loads = [
        pltpu.make_async_copy(source, target, in_sem.at[i])
        for i, (source, target) in enumerate(
            (
                (overflow_q, small_q),
                (key_pool, keys),
                (value_pool, values),
                (prefill_q, queries),
            )
        )
    ]
    for load in loads + tables:
        load.start()

    barrier = pltpu.get_barrier_semaphore()

    def greet_replica(i, _):
        pl.semaphore_signal(
            barrier, inc=1, device_id={"replica": lax.rem(me_r + i, n_rep)}, device_id_type=MESH
        )
        return 0

    def greet_tensor(i, _):
        pl.semaphore_signal(
            barrier, inc=1, device_id={"tensor": lax.rem(me_t + i, n_ten)}, device_id_type=MESH
        )
        return 0

    lax.fori_loop(1, n_rep, greet_replica, 0)
    lax.fori_loop(1, n_ten, greet_tensor, 0)

    for table in tables:
        table.wait()
    loads[0].wait()
    n_over = overflow_q.shape[0]
    n_dec = decode_q.shape[0]
    small_rows[0:n_over, :] = small_q[...].astype(F32)
    small_rows[n_over:, :] = jnp.zeros((8, GROUP * D), F32)
    small_rows[n_over : n_over + n_dec, :] = decode_held[...].astype(F32)
    loads[1].wait()
    loads[2].wait()

    row_slot = iota((64, 128), 0) % 8
    lane = iota((64, 128), 1)
    dec_pages = decode_pages.shape[1]
    attended = []
    for g in range(n_over // 8 + 1):
        q = jnp.concatenate(
            [small_rows[g * 8 : (g + 1) * 8, h * D : (h + 1) * D] for h in range(GROUP)], axis=0
        ).astype(BF16)
        pages, owner, limit = [], [], []
        for i in range(8):
            if g < n_over // 8:
                pages.append(overflow_pages[g * 8 + i])
                owner.append(i)
                limit.append(overflow_len[g * 8 + i])
            else:
                pages.append(decode_pages[i // dec_pages, i % dec_pages])
                owner.append(i // dec_pages)
                limit.append(decode_len[i // dec_pages] - (i % dec_pages) * PAGE)
        k = jnp.concatenate([keys[p] for p in pages], axis=0)
        v = jnp.concatenate([values[p] for p in pages], axis=0)
        s = tiles(dot_t(q, k))
        s = [
            jnp.where((row_slot == owner[i]) & (lane < limit[i]), s[i] * SCALE, NEG)
            for i in range(8)
        ]
        m = jnp.max(functools.reduce(jnp.maximum, s), axis=1, keepdims=True)
        p = [jnp.exp2(x - m) for x in s]
        total = jnp.sum(functools.reduce(jnp.add, p), axis=1, keepdims=True)
        o = jnp.dot(
            jnp.concatenate([x.astype(BF16) for x in p], axis=1), v, preferred_element_type=F32
        )
        attended.append((o / total).astype(BF16))
    last = attended[-1].astype(F32)
    for h in range(GROUP):
        decode_out[:, h * D : (h + 1) * D] = last[h * 8 : h * 8 + n_dec, :].astype(BF16)

    width = 64 * (n_over // 8)
    column = iota((1, width), 1)
    request = (column // 64) * 8 + column % 8
    dest = jnp.full((1, width), -1, jnp.int32)
    for j in range(n_over):
        dest = jnp.where(request == j, overflow_dest[j], dest)
    target = iota((n_rep * 8, width), 0)
    pick = (dest * 8 + (column // 8) % 8 == target).astype(F32).astype(BF16)
    sent = jnp.dot(pick, jnp.concatenate(attended[:-1], axis=0), preferred_element_type=F32)
    send_rows[...] = sent.reshape(n_rep, 8, D).astype(BF16)
    kept = pltpu.make_async_copy(send_rows.at[me_r], moved_rows.at[me_r], kept_sem)
    kept.start()

    def send_row(i, _):
        to = lax.rem(me_r + i, n_rep)
        pltpu.make_async_remote_copy(
            src_ref=send_rows.at[to],
            dst_ref=moved_rows.at[me_r],
            send_sem=row_send,
            recv_sem=row_recv,
            device_id={"replica": to},
            device_id_type=MESH,
        ).start()
        return 0

    def gather(i, _):
        at = pl.ds(pl.multiple_of(i * PAGE, PAGE), PAGE)
        listed = prefill_pages[0, i]
        page = keys[listed]
        key_rows[at, 0:D] = page
        key_rows[at, D : 2 * D] = page
        value_rows[at, 0:D] = values[listed]
        value_rows[at, D : 2 * D] = jnp.ones((PAGE, D), BF16)
        return 0

    lax.fori_loop(0, span // PAGE, gather, 0)
    loads[3].wait()

    chunks = [(o, min(CHUNK, span - o)) for o in range(0, span, CHUNK)]
    scratch = (score_a, score_b)
    me_x = me_t // 2

    def block_copy(at, to):
        offset = pl.multiple_of((to % 2) * part, 16)
        return pltpu.make_async_remote_copy(
            src_ref=blocks.at[at, pl.ds(offset, part), :],
            dst_ref=prefill_out.at[:, pl.ds(pl.multiple_of(me_t * GROUP * D, GROUP * D), GROUP * D)],
            send_sem=block_send.at[to],
            recv_sem=block_recv.at[me_t],
            device_id={"tensor": to},
            device_id_type=MESH,
        )

    def chip_of(step):
        return lax.rem(me_x + jnp.where(step < 2, 2 - step, 9 - 3 * step), chips)

    def send_block(step):
        for core in range(2):
            to = chip_of(step) * 2 + core

            @pl.when(to != me_t)
            def _():
                block_copy(step, to).start()

    z = lax.rem(me_r, depth_z)
    hold = jnp.where(z < 4, 3, jnp.where(z < 8, 1, 0))

    def block(step, _):
        @pl.when(step == hold)
        def _():
            pl.semaphore_wait(barrier, n_rep + n_ten - 2)
            lax.fori_loop(1, n_rep, send_row, 0)

            def send_held(i, _):
                send_block(i)
                return 0

            lax.fori_loop(0, step, send_held, 0)

        chip = chip_of(step)
        at = pl.ds(pl.multiple_of(chip * pair, pair), pair)
        q = jnp.concatenate([queries[at, h * D : (h + 1) * D] for h in range(GROUP)], axis=0)
        q = q.astype(F32) * SCALE
        high = q.astype(BF16)
        q = jnp.concatenate([high, (q - high.astype(F32)).astype(BF16)], axis=1)
        peak = [None] * len(chunks)

        def scores(j):
            o, w = chunks[j]
            s = dot_t(q, key_rows[o : o + w, :])
            if o + w > prior:
                token = iota((rows, w), 0) % pair + chip * pair
                s = jnp.where(iota((rows, w), 1) + (o - prior) <= token, s, NEG)
            m = jnp.max(functools.reduce(jnp.maximum, tiles(s)), axis=1, keepdims=True)
            m = jnp.broadcast_to(m, (rows, 128))
            peak[j] = m if j == 0 else jnp.maximum(peak[j - 1], m)
            scratch[j % 2][:, :w] = s

        def weigh(j, acc):
            o, w = chunks[j]
            p = [jnp.exp2(x - peak[j]).astype(BF16) for x in tiles(scratch[j % 2][:, :w])]
            o = jnp.dot(
                jnp.concatenate(p, axis=1), value_rows[o : o + w, :], preferred_element_type=F32
            )
            if acc is None:
                return o
            shrink = jnp.exp2(peak[j - 1] - peak[j])
            return jnp.concatenate([x * shrink for x in tiles(acc)], axis=1) + o

        acc = None
        for j in range(len(chunks) + 1):
            if j < len(chunks):
                scores(j)
            if j > 0:
                acc = weigh(j - 1, acc)
        out = (acc[:, :D] / acc[:, D:]).astype(BF16)
        for h in range(GROUP):
            blocks[step, :, h * D : (h + 1) * D] = out[h * pair : (h + 1) * pair, :]

        @pl.when(step >= hold)
        def _():
            send_block(step)

        return 0

    lax.fori_loop(0, chips, block, 0)

    own = pltpu.make_async_copy(
        blocks.at[chips - 1, pl.ds(pl.multiple_of((me_t % 2) * part, 16), part), :],
        prefill_out.at[:, pl.ds(pl.multiple_of(me_t * GROUP * D, GROUP * D), GROUP * D)],
        own_sem,
    )
    own.start()

    kept.wait()
    rest = moved_rows.at[0 : n_rep - 1]
    pltpu.make_async_copy(rest, rest, row_recv).wait()
    pltpu.make_async_copy(send_rows.at[0 : n_rep - 1], send_rows.at[0 : n_rep - 1], row_send).wait()
    own.wait()

    def finish(i, _):
        other = lax.rem(me_t + i, n_ten)
        arrived = prefill_out.at[
            :, pl.ds(pl.multiple_of(other * GROUP * D, GROUP * D), GROUP * D)
        ]
        pltpu.make_async_copy(arrived, arrived, block_recv.at[other]).wait()
        left = blocks.at[0, 0:part, :]
        pltpu.make_async_copy(left, left, block_send.at[other]).wait()
        return 0

    lax.fori_loop(1, n_ten, finish, 0)


def place_kernel(prefill, decode, moved, prefill_out, decode_out, moved_out, wide, flat, sem):
    n = moved.shape[0]
    writes = [
        pltpu.make_async_copy(prefill, prefill_out, sem.at[0]),
        pltpu.make_async_copy(decode, decode_out, sem.at[1]),
        pltpu.make_async_copy(flat, moved_out, sem.at[2]),
    ]
    writes[0].start()
    writes[1].start()
    wide[...] = moved[...].astype(F32).reshape(n * 8, D)
    for h in range(GROUP):
        flat[:, h * D : (h + 1) * D] = wide[pl.ds(h, n, stride=8), :].astype(BF16)
    writes[2].start()
    for write in writes:
        write.wait()


def place(prefill, decode, moved):
    n = moved.shape[0]
    return pl.pallas_call(
        place_kernel,
        out_shape=(
            jax.ShapeDtypeStruct(prefill.shape, BF16),
            jax.ShapeDtypeStruct(decode.shape, BF16),
            jax.ShapeDtypeStruct((n, GROUP * D), BF16),
        ),
        in_specs=[pl.BlockSpec(memory_space=pltpu.VMEM)] * 3,
        out_specs=(pl.BlockSpec(memory_space=pltpu.HBM),) * 3,
        scratch_shapes=[
            pltpu.VMEM((n * 8, D), F32),
            pltpu.VMEM((n, GROUP * D), BF16),
            pltpu.SemaphoreType.DMA((3,)),
        ],
        compiler_params=pltpu.CompilerParams(vmem_limit_bytes=PLACE_VMEM),
    )(prefill, decode, moved)


def per_device(
    prefill_q,
    decode_q,
    overflow_q,
    key_pool,
    value_pool,
    prefill_pages,
    decode_pages,
    decode_len,
    overflow_pages,
    overflow_len,
    overflow_dest,
):
    n_rep, n_ten = lax.axis_size("replica"), lax.axis_size("tensor")
    tokens, width = prefill_q.shape
    span = prefill_pages.shape[1] * PAGE
    rows = 2 * tokens // n_ten * GROUP
    n_over = overflow_q.shape[0]
    key_pool = key_pool.reshape(-1, PAGE, D)
    value_pool = value_pool.reshape(-1, PAGE, D)
    vmem = pl.BlockSpec(memory_space=pltpu.VMEM)
    hbm = pl.BlockSpec(memory_space=pltpu.HBM)
    free = pl.BlockSpec(memory_space=pl.ANY)
    raw = pl.pallas_call(
        functools.partial(kernel, (n_rep, n_ten, 16)),
        out_shape=(
            jax.ShapeDtypeStruct((tokens // n_ten, width * n_ten), BF16),
            jax.ShapeDtypeStruct(decode_q.shape, BF16),
            jax.ShapeDtypeStruct((n_rep, 8, D), BF16),
        ),
        in_specs=[hbm] * 11,
        out_specs=(free, vmem, free),
        scratch_shapes=[
            pltpu.SMEM(prefill_pages.shape, jnp.int32),
            pltpu.SMEM(decode_pages.shape, jnp.int32),
            pltpu.SMEM(decode_len.shape, jnp.int32),
            pltpu.SMEM(overflow_pages.shape, jnp.int32),
            pltpu.SMEM(overflow_len.shape, jnp.int32),
            pltpu.SMEM(overflow_dest.shape, jnp.int32),
            pltpu.VMEM(decode_q.shape, BF16),
            pltpu.VMEM(key_pool.shape, BF16),
            pltpu.VMEM(key_pool.shape, BF16),
            pltpu.VMEM((tokens, width), BF16),
            pltpu.VMEM((n_over, width), BF16),
            pltpu.VMEM((n_over + 8, width), F32),
            pltpu.VMEM((span, 2 * D), BF16),
            pltpu.VMEM((span, 2 * D), BF16),
            pltpu.VMEM((rows, CHUNK), F32),
            pltpu.VMEM((rows, CHUNK), F32),
            pltpu.VMEM((n_ten // 2, 2 * tokens // n_ten, width), BF16),
            pltpu.VMEM((n_rep, 8, D), BF16),
            pltpu.SemaphoreType.DMA((7,)),
            pltpu.SemaphoreType.DMA((4,)),
            pltpu.SemaphoreType.DMA((n_ten,)),
            pltpu.SemaphoreType.DMA((n_ten,)),
            pltpu.SemaphoreType.DMA,
            pltpu.SemaphoreType.DMA,
            pltpu.SemaphoreType.DMA,
            pltpu.SemaphoreType.DMA,
        ],
        compiler_params=pltpu.CompilerParams(
            collective_id=0, has_side_effects=True, vmem_limit_bytes=ATTEND_VMEM
        ),
    )(
        *(
            pltpu.with_memory_space_constraint(x, pltpu.HBM)
            for x in (
                prefill_pages,
                decode_pages,
                decode_len,
                overflow_pages,
                overflow_len,
                overflow_dest,
                prefill_q,
                decode_q,
                overflow_q,
                key_pool,
                value_pool,
            )
        )
    )
    return place(*raw)


def solution(mesh):
    both = P("replica", "tensor")
    in_specs = (both,) * 5 + (P("replica", None),) * 2 + (P("replica"),) * 4
    out_specs = (P(("replica", "tensor"), None), both, both)
    return jax.shard_map(
        per_device, mesh=mesh, in_specs=in_specs, out_specs=out_specs, check_vma=False
    )
```

```python
import functools
import math

import jax
import jax.numpy as jnp
from jax import lax
from jax.experimental import pallas as pl
from jax.experimental.pallas import tpu as pltpu
from jax.sharding import PartitionSpec as P

D = 128
PAGE = 128
GROUP = 8
SCALE = math.log2(math.e) / math.sqrt(D)
NEG = -1e30
CHUNK = 1024
ATTEND_VMEM = 24 << 20
PLACE_VMEM = 8 << 20
MESH = pl.DeviceIdType.MESH
BF16 = jnp.bfloat16
F32 = jnp.float32


def tiles(x):
    return [x[:, i : i + 128] for i in range(0, x.shape[1], 128)]


def dot_t(a, b):
    return lax.dot_general(a, b, (((1,), (1,)), ((), ())), preferred_element_type=F32)


def iota(shape, axis):
    return lax.broadcasted_iota(jnp.int32, shape, axis)


def kernel(
    sizes,
    prefill_pages_hbm,
    decode_pages_hbm,
    decode_len_hbm,
    overflow_pages_hbm,
    overflow_len_hbm,
    overflow_dest_hbm,
    prefill_q,
    decode_q,
    overflow_q,
    key_pool,
    value_pool,
    prefill_out,
    decode_out,
    moved_rows,
    prefill_pages,
    decode_pages,
    decode_len,
    overflow_pages,
    overflow_len,
    overflow_dest,
    decode_held,
    keys,
    values,
    queries,
    small_q,
    small_rows,
    key_rows,
    value_rows,
    score_a,
    score_b,
    blocks,
    send_rows,
    table_sem,
    in_sem,
    block_send,
    block_recv,
    own_sem,
    kept_sem,
    row_send,
    row_recv,
    everyone,
    group,
):
    n_rep, n_ten, depth_z = sizes
    me_r, me_t = lax.axis_index("replica"), lax.axis_index("tensor")
    span = key_rows.shape[0]
    tokens = queries.shape[0]
    part = tokens // n_ten
    pair = 2 * part
    rows = pair * GROUP
    prior = span - tokens
    chips = n_ten // 2

    tables = [
        pltpu.make_async_copy(source, target, table_sem.at[i])
        for i, (source, target) in enumerate(
            (
                (prefill_pages_hbm, prefill_pages),
                (decode_pages_hbm, decode_pages),
                (decode_len_hbm, decode_len),
                (overflow_pages_hbm, overflow_pages),
                (overflow_len_hbm, overflow_len),
                (overflow_dest_hbm, overflow_dest),
                (decode_q, decode_held),
            )
        )
    ]
    loads = [
        pltpu.make_async_copy(source, target, in_sem.at[i])
        for i, (source, target) in enumerate(
            (
                (overflow_q, small_q),
                (key_pool, keys),
                (value_pool, values),
                (prefill_q, queries),
            )
        )
    ]

    barrier = pltpu.get_barrier_semaphore()

    y, z = me_r // depth_z, lax.rem(me_r, depth_z)
    n_y = n_rep // depth_z
    host = n_ten - 1
    helper = n_ten - 2
    hosts = me_t == host
    hold = jnp.where(z < 4, 4, jnp.where(z < 8, 2, 0))

    def to_replicas(act):
        def body(i, _):
            to = lax.rem(y + lax.rem(i, n_y), n_y) * depth_z + i // n_y
            pl.when(to != me_r)(lambda: act(to))
            return 0

        lax.fori_loop(0, n_rep, body, 0)

    def greet_replica(to):
        pl.semaphore_signal(
            barrier, inc=1, device_id={"replica": to, "tensor": jnp.minimum(me_t, helper)}, device_id_type=MESH
        )

    to_replicas(greet_replica)

    @pl.when(jnp.logical_not(hosts))
    def _():
        pl.semaphore_signal(barrier, inc=1, device_id={"tensor": host}, device_id_type=MESH)

    for load in loads + tables:
        load.start()

    for table in tables:
        table.wait()
    loads[0].wait()
    n_over = overflow_q.shape[0]
    n_dec = decode_q.shape[0]
    small_rows[0:n_over, :] = small_q[...].astype(F32)
    small_rows[n_over:, :] = jnp.zeros((8, GROUP * D), F32)
    small_rows[n_over : n_over + n_dec, :] = decode_held[...].astype(F32)
    loads[1].wait()
    loads[2].wait()

    row_slot = iota((64, 128), 0) % 8
    lane = iota((64, 128), 1)
    dec_pages = decode_pages.shape[1]
    attended = []
    for g in range(n_over // 8 + 1):
        q = jnp.concatenate(
            [small_rows[g * 8 : (g + 1) * 8, h * D : (h + 1) * D] for h in range(GROUP)], axis=0
        ).astype(BF16)
        pages, owner, limit = [], [], []
        for i in range(8):
            if g < n_over // 8:
                pages.append(overflow_pages[g * 8 + i])
                owner.append(i)
                limit.append(overflow_len[g * 8 + i])
            else:
                pages.append(decode_pages[i // dec_pages, i % dec_pages])
                owner.append(i // dec_pages)
                limit.append(decode_len[i // dec_pages] - (i % dec_pages) * PAGE)
        k = jnp.concatenate([keys[p] for p in pages], axis=0)
        v = jnp.concatenate([values[p] for p in pages], axis=0)
        s = tiles(dot_t(q, k))
        s = [
            jnp.where((row_slot == owner[i]) & (lane < limit[i]), s[i] * SCALE, NEG)
            for i in range(8)
        ]
        m = jnp.max(functools.reduce(jnp.maximum, s), axis=1, keepdims=True)
        p = [jnp.exp2(x - m) for x in s]
        total = jnp.sum(functools.reduce(jnp.add, p), axis=1, keepdims=True)
        o = jnp.dot(
            jnp.concatenate([x.astype(BF16) for x in p], axis=1), v, preferred_element_type=F32
        )
        attended.append((o / total).astype(BF16))
    last = attended[-1].astype(F32)
    for h in range(GROUP):
        decode_out[:, h * D : (h + 1) * D] = last[h * 8 : h * 8 + n_dec, :].astype(BF16)

    width = 64 * (n_over // 8)
    column = iota((1, width), 1)
    request = (column // 64) * 8 + column % 8
    dest = jnp.full((1, width), -1, jnp.int32)
    for j in range(n_over):
        dest = jnp.where(request == j, overflow_dest[j], dest)
    target = iota((n_rep * 8, width), 0)
    pick = (dest * 8 + (column // 8) % 8 == target).astype(F32).astype(BF16)
    sent = jnp.dot(pick, jnp.concatenate(attended[:-1], axis=0), preferred_element_type=F32)
    send_rows[...] = sent.reshape(n_rep, 8, D).astype(BF16)
    kept = pltpu.make_async_copy(send_rows.at[me_r], moved_rows.at[me_r], kept_sem)
    kept.start()

    def send_row(to):
        pltpu.make_async_remote_copy(
            src_ref=send_rows.at[to],
            dst_ref=moved_rows.at[me_r],
            send_sem=row_send,
            recv_sem=row_recv,
            device_id={"replica": to},
            device_id_type=MESH,
        ).start()

    def gather(i, _):
        at = pl.ds(pl.multiple_of(i * PAGE, PAGE), PAGE)
        listed = prefill_pages[0, i]
        page = keys[listed]
        key_rows[at, 0:D] = page
        key_rows[at, D : 2 * D] = page
        value_rows[at, 0:D] = values[listed]
        value_rows[at, D : 2 * D] = jnp.ones((PAGE, D), BF16)
        return 0

    lax.fori_loop(0, span // PAGE, gather, 0)
    loads[3].wait()

    chunks = [(o, min(CHUNK, span - o)) for o in range(0, span, CHUNK)]
    scratch = (score_a, score_b)
    me_x = me_t // 2

    def block_copy(at, to):
        offset = pl.multiple_of((to % 2) * part, 16)
        return pltpu.make_async_remote_copy(
            src_ref=blocks.at[at, pl.ds(offset, part), :],
            dst_ref=prefill_out.at[:, pl.ds(pl.multiple_of(me_t * GROUP * D, GROUP * D), GROUP * D)],
            send_sem=block_send.at[to],
            recv_sem=block_recv.at[me_t],
            device_id={"tensor": to},
            device_id_type=MESH,
        )

    def chip_of(step):
        return lax.rem(me_x + jnp.where(step < 2, 2 - step, 9 - 3 * step), chips)

    def send_block(step):
        for core in range(2):
            to = chip_of(step) * 2 + core

            @pl.when(to != me_t)
            def _():
                block_copy(step, to).start()

    def tell(i, _):
        pl.semaphore_signal(group, inc=1, device_id={"tensor": i}, device_id_type=MESH)
        return 0

    def meet_group():
        @pl.when(hosts)
        def _():
            pl.semaphore_wait(barrier, n_ten - 1)
            lax.fori_loop(0, host, tell, 0)

        @pl.when(jnp.logical_not(hosts))
        def _():
            pl.semaphore_wait(group, 1)

    def meet():
        @pl.when(me_t < helper)
        def _():
            pl.semaphore_wait(barrier, n_rep - 1)

        @pl.when(me_t == helper)
        def _():
            pl.semaphore_wait(barrier, 2 * (n_rep - 1))
            pl.semaphore_signal(everyone, inc=1, device_id={"tensor": host}, device_id_type=MESH)

        @pl.when(hosts)
        def _():
            pl.semaphore_wait(everyone, 1)

        to_replicas(send_row)

    def block(step, _):
        at_once = hosts | (hold == 0)
        pl.when((step == 0) & at_once)(meet_group)
        pl.when(step == hold)(meet)
        chip = chip_of(step)
        at = pl.ds(pl.multiple_of(chip * pair, pair), pair)
        q = jnp.concatenate([queries[at, h * D : (h + 1) * D] for h in range(GROUP)], axis=0)
        q = q.astype(F32) * SCALE
        high = q.astype(BF16)
        q = jnp.concatenate([high, (q - high.astype(F32)).astype(BF16)], axis=1)
        peak = [None] * len(chunks)

        def scores(j):
            o, w = chunks[j]
            s = dot_t(q, key_rows[o : o + w, :])
            if o + w > prior:
                token = iota((rows, w), 0) % pair + chip * pair
                s = jnp.where(iota((rows, w), 1) + (o - prior) <= token, s, NEG)
            m = jnp.max(functools.reduce(jnp.maximum, tiles(s)), axis=1, keepdims=True)
            m = jnp.broadcast_to(m, (rows, 128))
            peak[j] = m if j == 0 else jnp.maximum(peak[j - 1], m)
            scratch[j % 2][:, :w] = s

        def weigh(j, acc):
            o, w = chunks[j]
            p = [jnp.exp2(x - peak[j]).astype(BF16) for x in tiles(scratch[j % 2][:, :w])]
            o = jnp.dot(
                jnp.concatenate(p, axis=1), value_rows[o : o + w, :], preferred_element_type=F32
            )
            if acc is None:
                return o
            shrink = jnp.exp2(peak[j - 1] - peak[j])
            return jnp.concatenate([x * shrink for x in tiles(acc)], axis=1) + o

        acc = None
        for j in range(len(chunks) + 1):
            if j < len(chunks):
                scores(j)
            if j > 0:
                acc = weigh(j - 1, acc)
        out = (acc[:, :D] / acc[:, D:]).astype(BF16)
        for h in range(GROUP):
            blocks[step, :, h * D : (h + 1) * D] = out[h * pair : (h + 1) * pair, :]

        pl.when((step == 0) & jnp.logical_not(at_once))(meet_group)
        send_block(step)
        return 0

    lax.fori_loop(0, chips, block, 0)
    pl.when(hold == chips)(meet)

    own = pltpu.make_async_copy(
        blocks.at[chips - 1, pl.ds(pl.multiple_of((me_t % 2) * part, 16), part), :],
        prefill_out.at[:, pl.ds(pl.multiple_of(me_t * GROUP * D, GROUP * D), GROUP * D)],
        own_sem,
    )
    own.start()

    kept.wait()
    rest = moved_rows.at[0 : n_rep - 1]
    pltpu.make_async_copy(rest, rest, row_recv).wait()
    pltpu.make_async_copy(send_rows.at[0 : n_rep - 1], send_rows.at[0 : n_rep - 1], row_send).wait()
    own.wait()

    def finish(i, _):
        other = lax.rem(me_t + i, n_ten)
        arrived = prefill_out.at[
            :, pl.ds(pl.multiple_of(other * GROUP * D, GROUP * D), GROUP * D)
        ]
        pltpu.make_async_copy(arrived, arrived, block_recv.at[other]).wait()
        left = blocks.at[0, 0:part, :]
        pltpu.make_async_copy(left, left, block_send.at[other]).wait()
        return 0

    lax.fori_loop(1, n_ten, finish, 0)


def place_kernel(prefill, decode, moved, prefill_out, decode_out, moved_out, wide, flat, sem):
    n = moved.shape[0]
    writes = [
        pltpu.make_async_copy(prefill, prefill_out, sem.at[0]),
        pltpu.make_async_copy(decode, decode_out, sem.at[1]),
        pltpu.make_async_copy(flat, moved_out, sem.at[2]),
    ]
    writes[0].start()
    writes[1].start()
    wide[...] = moved[...].astype(F32).reshape(n * 8, D)
    for h in range(GROUP):
        flat[:, h * D : (h + 1) * D] = wide[pl.ds(h, n, stride=8), :].astype(BF16)
    writes[2].start()
    for write in writes:
        write.wait()


def place(prefill, decode, moved):
    n = moved.shape[0]
    return pl.pallas_call(
        place_kernel,
        out_shape=(
            jax.ShapeDtypeStruct(prefill.shape, BF16),
            jax.ShapeDtypeStruct(decode.shape, BF16),
            jax.ShapeDtypeStruct((n, GROUP * D), BF16),
        ),
        in_specs=[pl.BlockSpec(memory_space=pltpu.VMEM)] * 3,
        out_specs=(pl.BlockSpec(memory_space=pltpu.HBM),) * 3,
        scratch_shapes=[
            pltpu.VMEM((n * 8, D), F32),
            pltpu.VMEM((n, GROUP * D), BF16),
            pltpu.SemaphoreType.DMA((3,)),
        ],
        compiler_params=pltpu.CompilerParams(vmem_limit_bytes=PLACE_VMEM),
    )(prefill, decode, moved)


def per_device(
    prefill_q,
    decode_q,
    overflow_q,
    key_pool,
    value_pool,
    prefill_pages,
    decode_pages,
    decode_len,
    overflow_pages,
    overflow_len,
    overflow_dest,
):
    n_rep, n_ten = lax.axis_size("replica"), lax.axis_size("tensor")
    tokens, width = prefill_q.shape
    span = prefill_pages.shape[1] * PAGE
    rows = 2 * tokens // n_ten * GROUP
    n_over = overflow_q.shape[0]
    key_pool = key_pool.reshape(-1, PAGE, D)
    value_pool = value_pool.reshape(-1, PAGE, D)
    vmem = pl.BlockSpec(memory_space=pltpu.VMEM)
    hbm = pl.BlockSpec(memory_space=pltpu.HBM)
    free = pl.BlockSpec(memory_space=pl.ANY)
    raw = pl.pallas_call(
        functools.partial(kernel, (n_rep, n_ten, 16)),
        out_shape=(
            jax.ShapeDtypeStruct((tokens // n_ten, width * n_ten), BF16),
            jax.ShapeDtypeStruct(decode_q.shape, BF16),
            jax.ShapeDtypeStruct((n_rep, 8, D), BF16),
        ),
        in_specs=[hbm] * 11,
        out_specs=(free, vmem, free),
        scratch_shapes=[
            pltpu.SMEM(prefill_pages.shape, jnp.int32),
            pltpu.SMEM(decode_pages.shape, jnp.int32),
            pltpu.SMEM(decode_len.shape, jnp.int32),
            pltpu.SMEM(overflow_pages.shape, jnp.int32),
            pltpu.SMEM(overflow_len.shape, jnp.int32),
            pltpu.SMEM(overflow_dest.shape, jnp.int32),
            pltpu.VMEM(decode_q.shape, BF16),
            pltpu.VMEM(key_pool.shape, BF16),
            pltpu.VMEM(key_pool.shape, BF16),
            pltpu.VMEM((tokens, width), BF16),
            pltpu.VMEM((n_over, width), BF16),
            pltpu.VMEM((n_over + 8, width), F32),
            pltpu.VMEM((span, 2 * D), BF16),
            pltpu.VMEM((span, 2 * D), BF16),
            pltpu.VMEM((rows, CHUNK), F32),
            pltpu.VMEM((rows, CHUNK), F32),
            pltpu.VMEM((n_ten // 2, 2 * tokens // n_ten, width), BF16),
            pltpu.VMEM((n_rep, 8, D), BF16),
            pltpu.SemaphoreType.DMA((7,)),
            pltpu.SemaphoreType.DMA((4,)),
            pltpu.SemaphoreType.DMA((n_ten,)),
            pltpu.SemaphoreType.DMA((n_ten,)),
            pltpu.SemaphoreType.DMA,
            pltpu.SemaphoreType.DMA,
            pltpu.SemaphoreType.DMA,
            pltpu.SemaphoreType.DMA,
            pltpu.SemaphoreType.REGULAR,
            pltpu.SemaphoreType.REGULAR,
        ],
        compiler_params=pltpu.CompilerParams(
            collective_id=0, has_side_effects=True, vmem_limit_bytes=ATTEND_VMEM
        ),
    )(
        *(
            pltpu.with_memory_space_constraint(x, pltpu.HBM)
            for x in (
                prefill_pages,
                decode_pages,
                decode_len,
                overflow_pages,
                overflow_len,
                overflow_dest,
                prefill_q,
                decode_q,
                overflow_q,
                key_pool,
                value_pool,
            )
        )
    )
    return place(*raw)


def solution(mesh):
    both = P("replica", "tensor")
    in_specs = (both,) * 5 + (P("replica", None),) * 2 + (P("replica"),) * 4
    out_specs = (P(("replica", "tensor"), None), both, both)
    return jax.shard_map(
        per_device, mesh=mesh, in_specs=in_specs, out_specs=out_specs, check_vma=False
    )
```

```python
import functools
import math

import jax
import jax.numpy as jnp
from jax import lax
from jax.experimental import pallas as pl
from jax.experimental.pallas import tpu as pltpu
from jax.sharding import PartitionSpec as P

D = 128
PAGE = 128
GROUP = 8
SCALE = math.log2(math.e) / math.sqrt(D)
NEG = -1e30
CHUNK = 1024
ATTEND_VMEM = 24 << 20
PLACE_VMEM = 8 << 20
MESH = pl.DeviceIdType.MESH
BF16 = jnp.bfloat16
F32 = jnp.float32


def tiles(x):
    return [x[:, i : i + 128] for i in range(0, x.shape[1], 128)]


def dot_t(a, b):
    return lax.dot_general(a, b, (((1,), (1,)), ((), ())), preferred_element_type=F32)


def iota(shape, axis):
    return lax.broadcasted_iota(jnp.int32, shape, axis)


def kernel(
    sizes,
    prefill_pages_hbm,
    decode_pages_hbm,
    decode_len_hbm,
    overflow_pages_hbm,
    overflow_len_hbm,
    overflow_dest_hbm,
    prefill_q,
    decode_q,
    overflow_q,
    key_pool,
    value_pool,
    prefill_out,
    decode_out,
    moved_rows,
    prefill_pages,
    decode_pages,
    decode_len,
    overflow_pages,
    overflow_len,
    overflow_dest,
    decode_held,
    keys,
    values,
    queries,
    small_q,
    small_rows,
    key_rows,
    value_rows,
    score_a,
    score_b,
    blocks,
    send_rows,
    table_sem,
    in_sem,
    block_send,
    block_recv,
    own_sem,
    kept_sem,
    row_send,
    row_recv,
    everyone,
    group,
):
    n_rep, n_ten, depth_z = sizes
    me_r, me_t = lax.axis_index("replica"), lax.axis_index("tensor")
    span = key_rows.shape[0]
    tokens = queries.shape[0]
    part = tokens // n_ten
    pair = 2 * part
    rows = pair * GROUP
    prior = span - tokens
    chips = n_ten // 2

    tables = [
        pltpu.make_async_copy(source, target, table_sem.at[i])
        for i, (source, target) in enumerate(
            (
                (prefill_pages_hbm, prefill_pages),
                (decode_pages_hbm, decode_pages),
                (decode_len_hbm, decode_len),
                (overflow_pages_hbm, overflow_pages),
                (overflow_len_hbm, overflow_len),
                (overflow_dest_hbm, overflow_dest),
                (decode_q, decode_held),
            )
        )
    ]
    loads = [
        pltpu.make_async_copy(source, target, in_sem.at[i])
        for i, (source, target) in enumerate(
            (
                (overflow_q, small_q),
                (key_pool, keys),
                (value_pool, values),
                (prefill_q, queries),
            )
        )
    ]

    for load in loads + tables:
        load.start()
    barrier = pltpu.get_barrier_semaphore()

    y, z = me_r // depth_z, lax.rem(me_r, depth_z)
    n_y = n_rep // depth_z
    host = n_ten - 1
    helper = n_ten - 2
    hosts = me_t == host
    hold = jnp.where(z < 3, 4, jnp.where(z < 5, 3, jnp.where(z < 8, 1, 0)))

    def to_replicas(act):
        def body(i, _):
            to = lax.rem(y + lax.rem(i, n_y), n_y) * depth_z + i // n_y
            pl.when(to != me_r)(lambda: act(to))
            return 0

        lax.fori_loop(0, n_rep, body, 0)

    def greet_replica(to):
        pl.semaphore_signal(
            barrier, inc=1, device_id={"replica": to, "tensor": jnp.minimum(me_t, helper)}, device_id_type=MESH
        )

    to_replicas(greet_replica)

    @pl.when(jnp.logical_not(hosts))
    def _():
        pl.semaphore_signal(barrier, inc=1, device_id={"tensor": host}, device_id_type=MESH)


    for table in tables:
        table.wait()
    loads[0].wait()
    n_over = overflow_q.shape[0]
    n_dec = decode_q.shape[0]
    small_rows[0:n_over, :] = small_q[...].astype(F32)
    small_rows[n_over:, :] = jnp.zeros((8, GROUP * D), F32)
    small_rows[n_over : n_over + n_dec, :] = decode_held[...].astype(F32)
    loads[1].wait()
    loads[2].wait()

    row_slot = iota((64, 128), 0) % 8
    lane = iota((64, 128), 1)
    dec_pages = decode_pages.shape[1]
    attended = []
    for g in range(n_over // 8 + 1):
        q = jnp.concatenate(
            [small_rows[g * 8 : (g + 1) * 8, h * D : (h + 1) * D] for h in range(GROUP)], axis=0
        ).astype(BF16)
        pages, owner, limit = [], [], []
        for i in range(8):
            if g < n_over // 8:
                pages.append(overflow_pages[g * 8 + i])
                owner.append(i)
                limit.append(overflow_len[g * 8 + i])
            else:
                pages.append(decode_pages[i // dec_pages, i % dec_pages])
                owner.append(i // dec_pages)
                limit.append(decode_len[i // dec_pages] - (i % dec_pages) * PAGE)
        k = jnp.concatenate([keys[p] for p in pages], axis=0)
        v = jnp.concatenate([values[p] for p in pages], axis=0)
        s = tiles(dot_t(q, k))
        s = [
            jnp.where((row_slot == owner[i]) & (lane < limit[i]), s[i] * SCALE, NEG)
            for i in range(8)
        ]
        m = jnp.max(functools.reduce(jnp.maximum, s), axis=1, keepdims=True)
        p = [jnp.exp2(x - m) for x in s]
        total = jnp.sum(functools.reduce(jnp.add, p), axis=1, keepdims=True)
        o = jnp.dot(
            jnp.concatenate([x.astype(BF16) for x in p], axis=1), v, preferred_element_type=F32
        )
        attended.append((o / total).astype(BF16))
    last = attended[-1].astype(F32)
    for h in range(GROUP):
        decode_out[:, h * D : (h + 1) * D] = last[h * 8 : h * 8 + n_dec, :].astype(BF16)

    width = 64 * (n_over // 8)
    column = iota((1, width), 1)
    request = (column // 64) * 8 + column % 8
    dest = jnp.full((1, width), -1, jnp.int32)
    for j in range(n_over):
        dest = jnp.where(request == j, overflow_dest[j], dest)
    target = iota((n_rep * 8, width), 0)
    pick = (dest * 8 + (column // 8) % 8 == target).astype(F32).astype(BF16)
    sent = jnp.dot(pick, jnp.concatenate(attended[:-1], axis=0), preferred_element_type=F32)
    send_rows[...] = sent.reshape(n_rep, 8, D).astype(BF16)
    kept = pltpu.make_async_copy(send_rows.at[me_r], moved_rows.at[me_r], kept_sem)
    kept.start()

    def send_row(to):
        pltpu.make_async_remote_copy(
            src_ref=send_rows.at[to],
            dst_ref=moved_rows.at[me_r],
            send_sem=row_send,
            recv_sem=row_recv,
            device_id={"replica": to},
            device_id_type=MESH,
        ).start()

    def gather(i, _):
        at = pl.ds(pl.multiple_of(i * PAGE, PAGE), PAGE)
        listed = prefill_pages[0, i]
        page = keys[listed]
        key_rows[at, 0:D] = page
        key_rows[at, D : 2 * D] = page
        value_rows[at, 0:D] = values[listed]
        value_rows[at, D : 2 * D] = jnp.ones((PAGE, D), BF16)
        return 0

    lax.fori_loop(0, span // PAGE, gather, 0)
    loads[3].wait()

    chunks = [(o, min(CHUNK, span - o)) for o in range(0, span, CHUNK)]
    scratch = (score_a, score_b)
    me_x = me_t // 2

    def block_copy(at, to):
        offset = pl.multiple_of((to % 2) * part, 16)
        return pltpu.make_async_remote_copy(
            src_ref=blocks.at[at, pl.ds(offset, part), :],
            dst_ref=prefill_out.at[:, pl.ds(pl.multiple_of(me_t * GROUP * D, GROUP * D), GROUP * D)],
            send_sem=block_send.at[to],
            recv_sem=block_recv.at[me_t],
            device_id={"tensor": to},
            device_id_type=MESH,
        )

    def chip_of(step):
        return lax.rem(me_x + jnp.where(step < 2, 2 - step, 9 - 3 * step), chips)

    def send_block(step):
        for core in range(2):
            to = chip_of(step) * 2 + core

            @pl.when(to != me_t)
            def _():
                block_copy(step, to).start()

    def tell(i, _):
        pl.semaphore_signal(group, inc=1, device_id={"tensor": i}, device_id_type=MESH)
        return 0

    def meet_group():
        @pl.when(hosts)
        def _():
            pl.semaphore_wait(barrier, n_ten - 1)
            lax.fori_loop(0, host, tell, 0)

        @pl.when(jnp.logical_not(hosts))
        def _():
            pl.semaphore_wait(group, 1)

    def meet():
        @pl.when(me_t < helper)
        def _():
            pl.semaphore_wait(barrier, n_rep - 1)

        @pl.when(me_t == helper)
        def _():
            pl.semaphore_wait(barrier, 2 * (n_rep - 1))
            pl.semaphore_signal(everyone, inc=1, device_id={"tensor": host}, device_id_type=MESH)

        @pl.when(hosts)
        def _():
            pl.semaphore_wait(everyone, 1)

        to_replicas(send_row)

    def block(step, _):
        at_once = hosts | (hold == 0)
        pl.when((step == 0) & at_once)(meet_group)
        pl.when(step == hold)(meet)
        chip = chip_of(step)
        at = pl.ds(pl.multiple_of(chip * pair, pair), pair)
        q = jnp.concatenate([queries[at, h * D : (h + 1) * D] for h in range(GROUP)], axis=0)
        q = q.astype(F32) * SCALE
        high = q.astype(BF16)
        q = jnp.concatenate([high, (q - high.astype(F32)).astype(BF16)], axis=1)
        peak = [None] * len(chunks)

        def scores(j):
            o, w = chunks[j]
            s = dot_t(q, key_rows[o : o + w, :])
            if o + w > prior:
                token = iota((rows, w), 0) % pair + chip * pair
                s = jnp.where(iota((rows, w), 1) + (o - prior) <= token, s, NEG)
            m = jnp.max(functools.reduce(jnp.maximum, tiles(s)), axis=1, keepdims=True)
            m = jnp.broadcast_to(m, (rows, 128))
            peak[j] = m if j == 0 else jnp.maximum(peak[j - 1], m)
            scratch[j % 2][:, :w] = s

        def weigh(j, acc):
            o, w = chunks[j]
            p = [jnp.exp2(x - peak[j]).astype(BF16) for x in tiles(scratch[j % 2][:, :w])]
            o = jnp.dot(
                jnp.concatenate(p, axis=1), value_rows[o : o + w, :], preferred_element_type=F32
            )
            if acc is None:
                return o
            shrink = jnp.exp2(peak[j - 1] - peak[j])
            return jnp.concatenate([x * shrink for x in tiles(acc)], axis=1) + o

        acc = None
        for j in range(len(chunks) + 1):
            if j < len(chunks):
                scores(j)
            if j > 0:
                acc = weigh(j - 1, acc)
        out = (acc[:, :D] / acc[:, D:]).astype(BF16)
        for h in range(GROUP):
            blocks[step, :, h * D : (h + 1) * D] = out[h * pair : (h + 1) * pair, :]

        pl.when((step == 0) & jnp.logical_not(at_once))(meet_group)
        send_block(step)
        return 0

    lax.fori_loop(0, chips, block, 0)
    pl.when(hold == chips)(meet)

    own = pltpu.make_async_copy(
        blocks.at[chips - 1, pl.ds(pl.multiple_of((me_t % 2) * part, 16), part), :],
        prefill_out.at[:, pl.ds(pl.multiple_of(me_t * GROUP * D, GROUP * D), GROUP * D)],
        own_sem,
    )
    own.start()

    kept.wait()
    rest = moved_rows.at[0 : n_rep - 1]
    pltpu.make_async_copy(rest, rest, row_recv).wait()
    pltpu.make_async_copy(send_rows.at[0 : n_rep - 1], send_rows.at[0 : n_rep - 1], row_send).wait()
    own.wait()

    def finish(i, _):
        other = lax.rem(me_t + i, n_ten)
        arrived = prefill_out.at[
            :, pl.ds(pl.multiple_of(other * GROUP * D, GROUP * D), GROUP * D)
        ]
        pltpu.make_async_copy(arrived, arrived, block_recv.at[other]).wait()
        left = blocks.at[0, 0:part, :]
        pltpu.make_async_copy(left, left, block_send.at[other]).wait()
        return 0

    lax.fori_loop(1, n_ten, finish, 0)


def place_kernel(prefill, decode, moved, prefill_out, decode_out, moved_out, wide, flat, sem):
    n = moved.shape[0]
    writes = [
        pltpu.make_async_copy(prefill, prefill_out, sem.at[0]),
        pltpu.make_async_copy(decode, decode_out, sem.at[1]),
        pltpu.make_async_copy(flat, moved_out, sem.at[2]),
    ]
    writes[0].start()
    writes[1].start()
    wide[...] = moved[...].astype(F32).reshape(n * 8, D)
    for h in range(GROUP):
        flat[:, h * D : (h + 1) * D] = wide[pl.ds(h, n, stride=8), :].astype(BF16)
    writes[2].start()
    for write in writes:
        write.wait()


def place(prefill, decode, moved):
    n = moved.shape[0]
    return pl.pallas_call(
        place_kernel,
        out_shape=(
            jax.ShapeDtypeStruct(prefill.shape, BF16),
            jax.ShapeDtypeStruct(decode.shape, BF16),
            jax.ShapeDtypeStruct((n, GROUP * D), BF16),
        ),
        in_specs=[pl.BlockSpec(memory_space=pltpu.VMEM)] * 3,
        out_specs=(pl.BlockSpec(memory_space=pltpu.HBM),) * 3,
        scratch_shapes=[
            pltpu.VMEM((n * 8, D), F32),
            pltpu.VMEM((n, GROUP * D), BF16),
            pltpu.SemaphoreType.DMA((3,)),
        ],
        compiler_params=pltpu.CompilerParams(vmem_limit_bytes=PLACE_VMEM),
    )(prefill, decode, moved)


def per_device(
    prefill_q,
    decode_q,
    overflow_q,
    key_pool,
    value_pool,
    prefill_pages,
    decode_pages,
    decode_len,
    overflow_pages,
    overflow_len,
    overflow_dest,
):
    n_rep, n_ten = lax.axis_size("replica"), lax.axis_size("tensor")
    tokens, width = prefill_q.shape
    span = prefill_pages.shape[1] * PAGE
    rows = 2 * tokens // n_ten * GROUP
    n_over = overflow_q.shape[0]
    key_pool = key_pool.reshape(-1, PAGE, D)
    value_pool = value_pool.reshape(-1, PAGE, D)
    vmem = pl.BlockSpec(memory_space=pltpu.VMEM)
    hbm = pl.BlockSpec(memory_space=pltpu.HBM)
    free = pl.BlockSpec(memory_space=pl.ANY)
    raw = pl.pallas_call(
        functools.partial(kernel, (n_rep, n_ten, 16)),
        out_shape=(
            jax.ShapeDtypeStruct((tokens // n_ten, width * n_ten), BF16),
            jax.ShapeDtypeStruct(decode_q.shape, BF16),
            jax.ShapeDtypeStruct((n_rep, 8, D), BF16),
        ),
        in_specs=[hbm] * 11,
        out_specs=(free, vmem, free),
        scratch_shapes=[
            pltpu.SMEM(prefill_pages.shape, jnp.int32),
            pltpu.SMEM(decode_pages.shape, jnp.int32),
            pltpu.SMEM(decode_len.shape, jnp.int32),
            pltpu.SMEM(overflow_pages.shape, jnp.int32),
            pltpu.SMEM(overflow_len.shape, jnp.int32),
            pltpu.SMEM(overflow_dest.shape, jnp.int32),
            pltpu.VMEM(decode_q.shape, BF16),
            pltpu.VMEM(key_pool.shape, BF16),
            pltpu.VMEM(key_pool.shape, BF16),
            pltpu.VMEM((tokens, width), BF16),
            pltpu.VMEM((n_over, width), BF16),
            pltpu.VMEM((n_over + 8, width), F32),
            pltpu.VMEM((span, 2 * D), BF16),
            pltpu.VMEM((span, 2 * D), BF16),
            pltpu.VMEM((rows, CHUNK), F32),
            pltpu.VMEM((rows, CHUNK), F32),
            pltpu.VMEM((n_ten // 2, 2 * tokens // n_ten, width), BF16),
            pltpu.VMEM((n_rep, 8, D), BF16),
            pltpu.SemaphoreType.DMA((7,)),
            pltpu.SemaphoreType.DMA((4,)),
            pltpu.SemaphoreType.DMA((n_ten,)),
            pltpu.SemaphoreType.DMA((n_ten,)),
            pltpu.SemaphoreType.DMA,
            pltpu.SemaphoreType.DMA,
            pltpu.SemaphoreType.DMA,
            pltpu.SemaphoreType.DMA,
            pltpu.SemaphoreType.REGULAR,
            pltpu.SemaphoreType.REGULAR,
        ],
        compiler_params=pltpu.CompilerParams(
            collective_id=0, has_side_effects=True, vmem_limit_bytes=ATTEND_VMEM
        ),
    )(
        *(
            pltpu.with_memory_space_constraint(x, pltpu.HBM)
            for x in (
                prefill_pages,
                decode_pages,
                decode_len,
                overflow_pages,
                overflow_len,
                overflow_dest,
                prefill_q,
                decode_q,
                overflow_q,
                key_pool,
                value_pool,
            )
        )
    )
    return place(*raw)


def solution(mesh):
    both = P("replica", "tensor")
    in_specs = (both,) * 5 + (P("replica", None),) * 2 + (P("replica"),) * 4
    out_specs = (P(("replica", "tensor"), None), both, both)
    return jax.shard_map(
        per_device, mesh=mesh, in_specs=in_specs, out_specs=out_specs, check_vma=False
    )
```
